32 devices in a mesh: ctx: 8 (over z, y), ch: 4 (over x, core).
Axes of the slice: x: 2, y: 2, z: 4, core: 2. Of those that a mesh axis runs over, the one named last changes fastest.
Arguments:
- queries: bfloat16 [2048, 4096], P('ctx', 'ch'), may hold values from -6 to 6
- keys: bfloat16 [2048, 4096], P('ctx', 'ch'), may hold values from -6 to 6
- values: bfloat16 [2048, 4096], P('ctx', 'ch'), may hold values from -6 to 6
- long_filter: float32 [2048, 4096], P('ctx', 'ch'), may hold values from -1.05 to 1.05
- short_filters: float32 [3, 3, 4096], P(None, None, 'ch'), may hold values from -3.6 to 3.6
- skip: float32 [4096], P('ch'), may hold values from -1 to 1
- w_out: bfloat16 [4096, 8192], P('ch'), may hold values from -0.09375 to 0.09375
- d_out: bfloat16 [2048, 8192], P('ctx', 'ch'), may hold values from -6 to 6
Outputs:
- d_queries: bfloat16 [2048, 4096], P('ctx', 'ch')
- d_keys: bfloat16 [2048, 4096], P('ctx', 'ch')
- d_values: bfloat16 [2048, 4096], P('ctx', 'ch')
- d_long: float32 [2048, 4096], P('ctx', 'ch')
- d_short: float32 [3, 3, 4096], P(None, None, 'ch')
- d_skip: float32 [4096], P('ch')
The draws below stay inside these ranges and needn't reach their ends.
All inputs are finite; a program needn't handle non-finite values.
Results may differ from the reference program's by a relative error of at most 0.0049.
Values may be sent and summed in bfloat16 or wider, within the bound.
A program may use at most 128 MiB of HBM per device.

```python
import jax
import jax.numpy as jnp
from jax import lax

D = 8192
CHANNELS = 4096
TAPS = 3
LENGTH = 2048


def draw_long_filter(key, part):
    rate_key = jax.random.fold_in(key, 11)
    noise_key = jax.random.fold_in(key, 23)
    low = jnp.log(jnp.float32(1.0) / (4.0 * LENGTH))
    high = jnp.log(jnp.float32(1.0) / 30.0)
    rates = jnp.exp(jax.random.uniform(rate_key, (CHANNELS,), jnp.float32, low, high))
    steps = jnp.arange(LENGTH, dtype=jnp.float32)
    scale = jnp.sqrt(jnp.maximum(2.0 * rates, 1.0 / LENGTH))
    envelope = jnp.exp(-steps[:, None] * rates[None, :]) * scale[None, :]
    noise = jnp.clip(jax.random.normal(noise_key, (LENGTH, CHANNELS), jnp.float32), -4.0, 4.0)
    return (noise * envelope).astype(jnp.float32)


def block_scale(stream_key, dims, shards, smallest, largest):
    factor_of, own = 1.0, jax.random.fold_in(stream_key, 6)
    for axis_at, shards_of in shards:
        steps = jnp.exp(jax.random.uniform(jax.random.fold_in(own, axis_at), (shards_of,), jnp.float32, smallest / len(shards), largest / len(shards)))
        factor_of = factor_of * jnp.repeat(steps, dims[axis_at] // shards_of).reshape([-1 if axis == axis_at else 1 for axis in range(len(dims))])
    return factor_of


def scatter_about(own_key, shape, scale, bound, pieces=(), kind=jnp.bfloat16):
    level = block_scale(own_key, shape, pieces, -0.22, 0.18) if pieces else 1.0
    array = jax.random.normal(own_key, shape, jnp.float32) * scale * level
    return jnp.minimum(jnp.maximum(array, -bound), bound).astype(kind)


def setup_inputs(seed: int = 0) -> dict:
    streams_of = jax.random.split(jax.random.key(seed), 9)
    return {
        "queries": scatter_about(streams_of[0], (LENGTH, CHANNELS), 1.0, 6.0, ((0, 8), (1, 4))),
        "keys": scatter_about(streams_of[1], (LENGTH, CHANNELS), 1.0, 6.0, ((0, 8), (1, 4))),
        "values": scatter_about(streams_of[2], (LENGTH, CHANNELS), 1.0, 6.0, ((0, 8), (1, 4))),
        "long_filter": draw_long_filter(jax.random.fold_in(streams_of[8], 71), 0),
        "short_filters": scatter_about(streams_of[4], (3, TAPS, CHANNELS), 0.6, 3.6, ((2, 4),), jnp.float32),
        "skip": jnp.clip(jax.random.uniform(streams_of[5], (CHANNELS,), jnp.float32, -1.0, 1.0) * block_scale(streams_of[5], (CHANNELS,), ((0, 4),), -0.4, 0.0), -1.0, 1.0),
        "w_out": scatter_about(streams_of[6], (CHANNELS, D), CHANNELS ** -0.5, 0.09375, ((0, 4),)),
        "d_out": scatter_about(streams_of[7], (LENGTH, D), 1.0, 6.0, ((0, 8), (1, 4))),
    }


def short_conv(stream, taps):
    padded = jnp.pad(stream, ((TAPS - 1, 0), (0, 0)))
    result = jnp.zeros(stream.shape, jnp.float32)
    for j in range(TAPS):
        result = result + taps[j][None, :] * padded[TAPS - 1 - j:TAPS - 1 - j + LENGTH]
    return result, padded


def back_conv(grad, taps):
    padded = jnp.pad(grad, ((0, TAPS - 1), (0, 0)))
    result = jnp.zeros(grad.shape, jnp.float32)
    for j in range(TAPS):
        result = result + taps[j][None, :] * padded[j:j + LENGTH]
    return result


def reference(queries, keys, values, long_filter, short_filters, skip, w_out, d_out):
    streams = [queries.astype(jnp.float32), keys.astype(jnp.float32), values.astype(jnp.float32)]
    filtered = []
    padded_in = []
    for s in range(3):
        out_s, pad_s = short_conv(streams[s], short_filters[s])
        filtered.append(out_s)
        padded_in.append(pad_s)
    mixed = filtered[1] * filtered[2]
    grad_o = jnp.dot(d_out, w_out.T, preferred_element_type=jnp.float32).astype(jnp.bfloat16)
    grad_o = lax.optimization_barrier(grad_o).astype(jnp.float32)
    grad_y = grad_o * filtered[0]
    total = 2 * LENGTH
    spec_mixed = jnp.fft.rfft(mixed, n=total, axis=0)
    spec_filter = jnp.fft.rfft(long_filter, n=total, axis=0)
    spec_grad = jnp.fft.rfft(grad_y, n=total, axis=0)
    conv_y = jnp.fft.irfft(spec_mixed * spec_filter, n=total, axis=0)[:LENGTH].astype(jnp.float32)
    conv_back = jnp.fft.irfft(spec_grad * jnp.conj(spec_filter), n=total, axis=0)[:LENGTH].astype(jnp.float32)
    d_long = jnp.fft.irfft(spec_grad * jnp.conj(spec_mixed), n=total, axis=0)[:LENGTH].astype(jnp.float32)
    y_full = conv_y + skip[None, :] * mixed
    grad_mixed = conv_back + skip[None, :] * grad_y
    d_skip = jnp.sum(grad_y * mixed, axis=0)
    grads = [grad_o * y_full, grad_mixed * filtered[2], grad_mixed * filtered[1]]
    short_rows = []
    for s in range(3):
        tap_rows = []
        for j in range(TAPS):
            tap_rows.append(jnp.sum(grads[s] * padded_in[s][TAPS - 1 - j:TAPS - 1 - j + LENGTH], axis=0))
        short_rows.append(jnp.stack(tap_rows))
    d_short = jnp.stack(short_rows)
    d_queries = back_conv(grads[0], short_filters[0]).astype(jnp.bfloat16)
    d_keys = back_conv(grads[1], short_filters[1]).astype(jnp.bfloat16)
    d_values = back_conv(grads[2], short_filters[2]).astype(jnp.bfloat16)
    return (d_queries, d_keys, d_values, d_long, d_short, d_skip)
```

```python
import functools
import math

import jax
import jax.numpy as jnp
import numpy as np
from jax import lax
from jax.experimental import pallas as pl
from jax.experimental.pallas import tpu as pltpu
from jax.sharding import PartitionSpec as P

PAD = 8
TAIL = 16
PARAMS = dict(vmem_limit_bytes=60 * 1024 * 1024)
F32 = jnp.float32
BF16 = jnp.bfloat16


def split_table(table):
    table = table.astype(np.float32)
    high = table.astype(BF16)
    low = (table - high.astype(np.float32)).astype(BF16)
    return np.concatenate([high[None], low[None]], axis=0)


def tables(block):
    freq = np.arange(block)[:, None]
    place = np.arange(block)[None, :]
    angle = (2 * freq + 1) * place % (4 * block) * (math.pi / (2 * block))
    forward = np.concatenate([np.cos(angle), -np.sin(angle)], axis=0)
    return split_table(forward), split_table(forward.T / block)


def shifted(block, axis, distance):
    devices = range(lax.axis_size(axis))
    route = [(i - distance, i) for i in devices if i - distance in devices]
    return lax.ppermute(block, axis, route)


def fill(scratch, before, own, after, rim):
    rows = own.shape[0]
    scratch[0:PAD, :] = jnp.zeros_like(scratch[0:PAD, :])
    scratch[PAD + rows :, :] = jnp.zeros_like(scratch[PAD + rows :, :])
    scratch[PAD - rim : PAD, :] = before.astype(F32)
    scratch[PAD : PAD + rows, :] = own.astype(F32)
    if after is not None:
        scratch[PAD + rows : PAD + rows + rim, :] = after.astype(F32)


def short(scratch, taps, rows, lanes, s):
    total = None
    for j in range(taps.shape[1]):
        term = taps[s, j : j + 1, lanes] * scratch[PAD - j : PAD - j + rows, :]
        total = term if total is None else total + term
    return total


def enter_kernel(pieces, k_ref, v_ref, before, long_ref, taps, mh_ref, ext):
    rows, width = k_ref.shape
    cw = width // pieces
    rim = before.shape[1]
    for c in range(pieces):
        lanes = slice(c * cw, (c + 1) * cw)
        fill(ext, before[1, :, lanes], k_ref[:, lanes], None, rim)
        keyed = short(ext, taps, rows, lanes, 1)
        fill(ext, before[2, :, lanes], v_ref[:, lanes], None, rim)
        mh_ref[c, 0] = (keyed * short(ext, taps, rows, lanes, 2)).astype(BF16)
        mh_ref[c, 1] = long_ref[:, lanes].astype(BF16)


def grad_kernel(pieces, q_ref, before, go_ref, taps, g_ref, ext):
    rows, width = q_ref.shape
    cw = width // pieces
    rim = before.shape[1]
    for c in range(pieces):
        lanes = slice(c * cw, (c + 1) * cw)
        fill(ext, before[0, :, lanes], q_ref[:, lanes], None, rim)
        g_ref[c] = (go_ref[:, lanes].astype(F32) * short(ext, taps, rows, lanes, 0)).astype(BF16)


def times(a, b):
    return a[0] * b[0] - a[1] * b[1], a[0] * b[1] + a[1] * b[0]


def conj_times(a, b):
    return a[0] * b[0] + a[1] * b[1], a[0] * b[1] - a[1] * b[0]


def add(a, b):
    return b if a is None else (a[0] + b[0], a[1] + b[1])


def spectra(table, blocks, spec):
    for at in range(0, len(blocks), 2):
        pair = blocks[at : at + 2]
        data = jnp.concatenate([ref[...] for ref, _, _ in pair], axis=1)
        out = jnp.dot(table[0], data, preferred_element_type=F32) + jnp.dot(
            table[1], data, preferred_element_type=F32
        )
        cw = data.shape[1] // len(pair)
        for p, (_, s, i) in enumerate(pair):
            spec[s, i] = out[:, p * cw : (p + 1) * cw]


def mix_spectra(spec, primed, held):
    count, rows2, cw = spec.shape[1:]
    half = rows2 // 2
    step = 8
    sign = 1.0 - 2.0 * (lax.broadcasted_iota(jnp.int32, (step, cw), 0) % 2).astype(F32)

    def primes(blocks):
        out = [blocks[0]]
        for d in range(1, count):
            re, im = blocks[d]
            old_re, old_im = blocks[d - 1]
            out.append((re - sign * old_im, im + sign * old_re))
        return out

    def chunk(r, carry):
        low = pl.ds(pl.multiple_of(r * step, step), step)
        high = pl.ds(pl.multiple_of(half + r * step, step), step)

        def load(s, i):
            return spec[s, i, low, :], spec[s, i, high, :]

        def save(s, i, value):
            spec[s, i, low, :] = value[0]
            spec[s, i, high, :] = value[1]

        if count <= 8:
            mixed = [load(0, i) for i in range(count)]
            taps = primes([load(1, i) for i in range(count)])
            for i in range(count):
                total = None
                for d in range(i + 1):
                    total = add(total, times(taps[d], mixed[i - d]))
                save(0, i, total)
            grads = [load(2, i) for i in range(count)]
            for b in range(count):
                total = None
                for e in range(count - b):
                    total = add(total, conj_times(taps[e], grads[b + e]))
                save(1, b, total)
            mixed = primes(mixed)
            for b in range(count):
                total = None
                for e in range(count - b):
                    total = add(total, conj_times(mixed[e], grads[b + e]))
                save(2, b, total)
            return carry

        for s in range(2):
            for d, value in enumerate(primes([load(s, i) for i in range(count)])):
                primed[s, d, 0] = value[0]
                primed[s, d, 1] = value[1]
        zero = jnp.zeros((step, cw), F32)

        def one(b, inner):
            def of_y(d, total):
                return add(total, times((primed[1, d, 0], primed[1, d, 1]), load(0, b - d)))

            def of_g(e, totals):
                grad = load(2, b + e)
                first = conj_times((primed[1, e, 0], primed[1, e, 1]), grad)
                second = conj_times((primed[0, e, 0], primed[0, e, 1]), grad)
                return add(totals[0], first), add(totals[1], second)

            held[0, b, 0], held[0, b, 1] = lax.fori_loop(0, b + 1, of_y, (zero, zero))
            first, second = lax.fori_loop(0, count - b, of_g, ((zero, zero), (zero, zero)))
            held[1, b, 0], held[1, b, 1] = first
            held[2, b, 0], held[2, b, 1] = second
            return inner

        lax.fori_loop(0, count, one, 0)
        for s in range(3):
            for b in range(count):
                save(s, b, (held[s, b, 0], held[s, b, 1]))
        return carry

    lax.fori_loop(0, half // step, chunk, 0)


def back_pair(table, values):
    data = jnp.concatenate(values, axis=1)
    high = data.astype(BF16)
    low = (data - high.astype(F32)).astype(BF16)
    out = (
        jnp.dot(table[0], high, preferred_element_type=F32)
        + jnp.dot(table[0], low, preferred_element_type=F32)
        + jnp.dot(table[1], high, preferred_element_type=F32)
    )
    cw = data.shape[1] // len(values)
    return [out[:, p * cw : (p + 1) * cw].astype(BF16) for p in range(len(values))]


def conv_kernel(mh_ref, g_ref, forward, inverse, out_ref, spec, primed, held):
    count, _, rows, cw = mh_ref.shape
    blocks = []
    for i in range(count):
        blocks += [(mh_ref.at[i, 0], 0, i), (mh_ref.at[i, 1], 1, i)]
    blocks += [(g_ref.at[i], 2, i) for i in range(count)]
    spectra(forward, blocks, spec)
    mix_spectra(spec, primed, held)
    base = (0, rows + TAIL, 2 * (rows + TAIL))
    for s in range(3):
        at = base[s]
        for i in range(0, count, 2):
            many = min(2, count - i)
            results = back_pair(inverse, [spec[s, i + p] for p in range(many)])
            for p, value in enumerate(results):
                out_ref[i + p, at : at + rows, :] = value
                if s < 2 and i + p > 0:
                    out_ref[i + p - 1, at + rows : at + rows + TAIL, :] = value[:TAIL]
        if s < 2:
            out_ref[count - 1, at + rows : at + rows + TAIL, :] = jnp.zeros((TAIL, cw), BF16)


def leave_kernel(pieces, q_ref, k_ref, v_ref, before, after, go_ref, go_after, taps, skip_ref,
                 got_ref, dq_ref, dk_ref, dv_ref, long_ref, sums_ref, ext, go_ext, grad_ext):
    rows, width = q_ref.shape
    cw = width // pieces
    rim = before.shape[1]
    tap_count = taps.shape[1]
    more = rows + PAD
    sums_ref[...] = jnp.zeros_like(sums_ref)
    for c in range(pieces):
        lanes = slice(c * cw, (c + 1) * cw)
        filtered = []
        for s, ref in enumerate((q_ref, k_ref, v_ref)):
            fill(ext.at[s], before[s, :, lanes], ref[:, lanes], after[s, :, lanes], rim)
            filtered.append(short(ext.at[s], taps, more, lanes, s))
        fill(go_ext, jnp.zeros((rim, cw), F32), go_ref[:, lanes], go_after[:, lanes], rim)
        grad_o = go_ext[PAD : PAD + more, :]
        mixed = filtered[1] * filtered[2]
        grad_y = grad_o * filtered[0]
        gain = skip_ref[:, lanes]
        y_full = got_ref[c, 0:more, :].astype(F32) + gain * mixed
        at = rows + TAIL
        grad_mixed = got_ref[c, at : at + more, :].astype(F32) + gain * grad_y
        grad_ext[0, 0:more, :] = grad_o * y_full
        grad_ext[1, 0:more, :] = grad_mixed * filtered[2]
        grad_ext[2, 0:more, :] = grad_mixed * filtered[1]
        long_ref[:, lanes] = got_ref[c, 2 * at : 2 * at + rows, :].astype(F32)
        for s, ref in enumerate((dq_ref, dk_ref, dv_ref)):
            total = None
            own = grad_ext[s, 0:rows, :]
            for j in range(tap_count):
                term = taps[s, j : j + 1, lanes] * grad_ext[s, j : j + rows, :]
                total = term if total is None else total + term
                stream = ext[s, PAD - j : PAD - j + rows, :]
                row = s * tap_count + j
                sums_ref[row : row + 1, lanes] = jnp.sum(own * stream, axis=0, keepdims=True)
            ref[:, lanes] = total.astype(BF16)
        row = 3 * tap_count
        sums_ref[row : row + 1, lanes] = jnp.sum(
            grad_y[0:rows] * mixed[0:rows], axis=0, keepdims=True
        )


def call(kernel, out_shape, scratch, *args, **params):
    return pl.pallas_call(
        kernel,
        out_shape=out_shape,
        in_specs=[pl.BlockSpec(memory_space=pltpu.VMEM)] * len(args),
        out_specs=jax.tree.map(lambda _: pl.BlockSpec(memory_space=pltpu.VMEM), out_shape),
        scratch_shapes=scratch,
        compiler_params=pltpu.CompilerParams(**PARAMS, **params),
    )(*args)


def per_device(queries, keys, values, long_filter, short_filters, skip, w_out, d_out):
    ctx = lax.axis_size("ctx")
    rows, width = queries.shape
    cw = width // ctx
    tap_count = short_filters.shape[1]
    rim = tap_count - 1
    ends = jnp.stack([queries[rows - rim :], keys[rows - rim :], values[rows - rim :]])
    starts = jnp.stack([queries[:rim], keys[:rim], values[:rim]])
    before = shifted(ends, "ctx", 1)
    after = shifted(starts, "ctx", -1)
    ext = pltpu.VMEM((rows + 4 * PAD, cw), F32)
    shape = jax.ShapeDtypeStruct
    mh = call(
        functools.partial(enter_kernel, ctx),
        shape((ctx, 2, rows, cw), BF16), [ext],
        keys, values, before, long_filter, short_filters,
    )
    mh = lax.all_to_all(mh, "ctx", split_axis=0, concat_axis=0, tiled=True)
    grad_o = lax.dot_general(
        lax.all_gather(d_out, "ch", axis=1, tiled=True),
        w_out,
        (((1,), (1,)), ((), ())),
        preferred_element_type=F32,
    ).astype(BF16)
    go_after = shifted(grad_o[:rim], "ctx", -1)
    g = call(
        functools.partial(grad_kernel, ctx),
        shape((ctx, rows, cw), BF16), [ext],
        queries, before, grad_o, short_filters,
    )
    g = lax.all_to_all(g, "ctx", split_axis=0, concat_axis=0, tiled=True)
    forward, inverse = tables(rows)
    spare = ctx if ctx > 8 else 1
    back = call(
        conv_kernel,
        shape((ctx, 3 * rows + 2 * TAIL, cw), BF16),
        [pltpu.VMEM((3, ctx, 2 * rows, cw), F32), pltpu.VMEM((2, spare, 2, 8, cw), F32),
         pltpu.VMEM((3, spare, 2, 8, cw), F32)],
        mh, g, jnp.asarray(forward), jnp.asarray(inverse),
    )
    back = lax.all_to_all(back, "ctx", split_axis=0, concat_axis=0, tiled=True)
    stream = shape((rows, width), BF16)
    dq, dk, dv, d_long, sums = call(
        functools.partial(leave_kernel, ctx),
        (stream, stream, stream, shape((rows, width), F32), shape((16, width), F32)),
        [pltpu.VMEM((3, rows + 4 * PAD, cw), F32), ext, pltpu.VMEM((3, rows + 4 * PAD, cw), F32)],
        queries, keys, values, before, after, grad_o, go_after, short_filters, skip[None], back,
    )
    sums = lax.psum(sums, "ctx")
    d_short = sums[: 3 * tap_count].reshape(3, tap_count, width)
    return dq, dk, dv, d_long, d_short, sums[3 * tap_count]


def solution(mesh):
    in_specs = (
        P("ctx", "ch"),
        P("ctx", "ch"),
        P("ctx", "ch"),
        P("ctx", "ch"),
        P(None, None, "ch"),
        P("ch"),
        P("ch", None),
        P("ctx", "ch"),
    )
    out_specs = (
        P("ctx", "ch"),
        P("ctx", "ch"),
        P("ctx", "ch"),
        P("ctx", "ch"),
        P(None, None, "ch"),
        P("ch"),
    )
    return jax.shard_map(
        per_device, mesh=mesh, in_specs=in_specs, out_specs=out_specs, check_vma=False
    )
```

```python
import functools
import math

import jax
import jax.numpy as jnp
import numpy as np
from jax import lax
from jax.experimental import pallas as pl
from jax.experimental.pallas import tpu as pltpu
from jax.sharding import PartitionSpec as P

PAD = 8
TAIL = 16
PARAMS = dict(vmem_limit_bytes=60 * 1024 * 1024)
F32 = jnp.float32
BF16 = jnp.bfloat16
MESH = pl.DeviceIdType.MESH


def split_table(table):
    table = table.astype(np.float32)
    high = table.astype(BF16)
    low = (table - high.astype(np.float32)).astype(BF16)
    return np.concatenate([high[None], low[None]], axis=0)


def tables(block):
    freq = np.arange(block)[:, None]
    place = np.arange(block)[None, :]
    angle = (2 * freq + 1) * place % (4 * block) * (math.pi / (2 * block))
    forward = np.concatenate([np.cos(angle), -np.sin(angle)], axis=0)
    return split_table(forward), split_table(forward.T / block)


def shifted(block, axis, distance):
    devices = range(lax.axis_size(axis))
    route = [(i - distance, i) for i in devices if i - distance in devices]
    return lax.ppermute(block, axis, route)


def fill(scratch, before, own, after, rim):
    rows = own.shape[0]
    scratch[0:PAD, :] = jnp.zeros_like(scratch[0:PAD, :])
    scratch[PAD + rows :, :] = jnp.zeros_like(scratch[PAD + rows :, :])
    scratch[PAD - rim : PAD, :] = before.astype(F32)
    scratch[PAD : PAD + rows, :] = own.astype(F32)
    if after is not None:
        scratch[PAD + rows : PAD + rows + rim, :] = after.astype(F32)


def short(scratch, taps, rows, lanes, s):
    total = None
    for j in range(taps.shape[1]):
        term = taps[s, j : j + 1, lanes] * scratch[PAD - j : PAD - j + rows, :]
        total = term if total is None else total + term
    return total


def enter_kernel(pieces, k_ref, v_ref, before, long_ref, taps, mh_ref, ext):
    rows, width = k_ref.shape
    cw = width // pieces
    rim = before.shape[1]
    for c in range(pieces):
        lanes = slice(c * cw, (c + 1) * cw)
        fill(ext, before[1, :, lanes], k_ref[:, lanes], None, rim)
        keyed = short(ext, taps, rows, lanes, 1)
        fill(ext, before[2, :, lanes], v_ref[:, lanes], None, rim)
        mh_ref[c, 0] = (keyed * short(ext, taps, rows, lanes, 2)).astype(BF16)
        mh_ref[c, 1] = long_ref[:, lanes].astype(BF16)


def times(a, b):
    return a[0] * b[0] - a[1] * b[1], a[0] * b[1] + a[1] * b[0]


def conj_times(a, b):
    return a[0] * b[0] + a[1] * b[1], a[0] * b[1] - a[1] * b[0]


def add(a, b):
    return b if a is None else (a[0] + b[0], a[1] + b[1])


def spectra(table, blocks, spec):
    for at in range(0, len(blocks), 2):
        pair = blocks[at : at + 2]
        data = jnp.concatenate([ref[...] for ref, _, _ in pair], axis=1)
        out = jnp.dot(table[0], data, preferred_element_type=F32) + jnp.dot(
            table[1], data, preferred_element_type=F32
        )
        cw = data.shape[1] // len(pair)
        for p, (_, s, i) in enumerate(pair):
            spec[s, i] = out[:, p * cw : (p + 1) * cw]


def mix_spectra(first, spec, held):
    count, rows2, cw = spec.shape[1:]
    half = rows2 // 2
    step = 8
    sign = 1.0 - 2.0 * (lax.broadcasted_iota(jnp.int32, (step, cw), 0) % 2).astype(F32)
    zero = jnp.zeros((step, cw), F32)

    def primes(blocks):
        out = [blocks[0]]
        for d in range(1, count):
            re, im = blocks[d]
            old_re, old_im = blocks[d - 1]
            out.append((re - sign * old_im, im + sign * old_re))
        return out

    def chunk(r, carry):
        low = pl.ds(pl.multiple_of(r * step, step), step)
        high = pl.ds(pl.multiple_of(half + r * step, step), step)

        def load(s, i):
            return spec[s, i, low, :], spec[s, i, high, :]

        def save(s, i, value):
            spec[s, i, low, :] = value[0]
            spec[s, i, high, :] = value[1]

        def primed(s):
            values = primes([load(s, i) for i in range(count)])
            for i in range(count):
                save(s, i, values[i])
            return values

        if count <= 8 and first:
            taps = primed(1)
            mixed = [load(0, i) for i in range(count)]
            for i in range(count):
                total = None
                for d in range(i + 1):
                    total = add(total, times(taps[d], mixed[i - d]))
                save(2, i, total)
            return carry
        if count <= 8:
            grads = [load(2, i) for i in range(count)]
            for s in (1, 0):
                taps = [load(s, i) for i in range(count)]
                if s == 0:
                    taps = primes(taps)
                for b in range(count):
                    total = None
                    for e in range(count - b):
                        total = add(total, conj_times(taps[e], grads[b + e]))
                    save(s, b, total)
            return carry
        if first:
            primed(1)

            def one(b, inner):
                def of_y(d, total):
                    return add(total, times(load(1, d), load(0, b - d)))

                save(2, b, lax.fori_loop(0, b + 1, of_y, (zero, zero)))
                return inner

            lax.fori_loop(0, count, one, 0)
            return carry
        primed(0)

        def both(b, inner):
            def of_g(e, totals):
                grad = load(2, b + e)
                return (
                    add(totals[0], conj_times(load(1, e), grad)),
                    add(totals[1], conj_times(load(0, e), grad)),
                )

            pair = lax.fori_loop(0, count - b, of_g, ((zero, zero), (zero, zero)))
            for s in range(2):
                held[s, b, 0], held[s, b, 1] = pair[s]
            return inner

        lax.fori_loop(0, count, both, 0)
        for b in range(count):
            save(1, b, (held[0, b, 0], held[0, b, 1]))
            save(0, b, (held[1, b, 0], held[1, b, 1]))
        return carry

    lax.fori_loop(0, half // step, chunk, 0)


def back_pair(table, values):
    data = jnp.concatenate(values, axis=1)
    high = data.astype(BF16)
    low = (data - high.astype(F32)).astype(BF16)
    out = (
        jnp.dot(table[0], high, preferred_element_type=F32)
        + jnp.dot(table[0], low, preferred_element_type=F32)
        + jnp.dot(table[1], high, preferred_element_type=F32)
    )
    cw = data.shape[1] // len(values)
    return [out[:, p * cw : (p + 1) * cw].astype(BF16) for p in range(len(values))]


def greet(axis, size, me):
    barrier = pltpu.get_barrier_semaphore()
    for o in range(1, size):
        peer = lax.rem(me + o, size)
        pl.semaphore_signal(barrier, inc=1, device_id={axis: peer}, device_id_type=MESH)
    pl.semaphore_wait(barrier, size - 1)


def send(source, target, send_sem, recv_sem, peer):
    return pltpu.make_async_remote_copy(
        src_ref=source,
        dst_ref=target,
        send_sem=send_sem,
        recv_sem=recv_sem,
        device_id={"ctx": peer},
        device_id_type=MESH,
    )


def far_first(size):
    return sorted(range(1, size), key=lambda o: abs(o - size // 2))


def conv_kernel(q_ref, before, go_ref, taps, mh_ref, forward, inverse, y_ref, b_ref, edge_ref,
                ext, g_tx, g_rx, y_tx, b_tx, spec, held, sent, came, edge_sem):
    count, _, rows, cw = mh_ref.shape
    rim = before.shape[1]
    me = lax.axis_index("ctx")
    greet("ctx", count, me)
    edge_rows = edge_ref.shape[0]
    previous = lax.rem(me + count - 1, count)
    edge = send(go_ref.at[0:edge_rows], edge_ref, edge_sem.at[0], edge_sem.at[1], previous)
    edge.start()
    for c in range(count):
        lanes = slice(c * cw, (c + 1) * cw)
        fill(ext, before[0, :, lanes], q_ref[:, lanes], None, rim)
        g_tx[c] = (go_ref[:, lanes].astype(F32) * short(ext, taps, rows, lanes, 0)).astype(BF16)

    def exchange(kind, source, target, peer):
        return send(
            source.at[peer], target.at[me], sent.at[kind, peer], came.at[kind, me], peer
        )

    def arrival(kind, source, target, peer):
        return send(
            source.at[peer], target.at[peer], sent.at[kind, peer], came.at[kind, peer], peer
        )

    peers = [lax.rem(me + o, count) for o in far_first(count)]
    for peer in peers:
        exchange(0, g_tx, g_rx, peer).start()
    g_rx[me] = g_tx[me]

    blocks = []
    for i in range(count):
        blocks += [(mh_ref.at[i, 0], 0, i), (mh_ref.at[i, 1], 1, i)]
    spectra(forward, blocks, spec)
    mix_spectra(True, spec, held)
    for i in range(0, count, 2):
        for p, value in enumerate(back_pair(inverse, [spec[2, i], spec[2, i + 1]])):
            y_tx[i + p, 0:rows, :] = value
            if i + p > 0:
                y_tx[i + p - 1, rows : rows + TAIL, :] = value[:TAIL]
    y_tx[count - 1, rows : rows + TAIL, :] = jnp.zeros((TAIL, cw), BF16)
    for peer in peers:
        exchange(1, y_tx, y_ref, peer).start()
    y_ref[me] = y_tx[me]

    for peer in peers:
        arrival(0, g_tx, g_rx, peer).wait_recv()
    spectra(forward, [(g_rx.at[i], 2, i) for i in range(count)], spec)
    mix_spectra(False, spec, held)

    def give(piece):
        @pl.when(piece != me)
        def _():
            exchange(2, b_tx, b_ref, piece).start()

        @pl.when(piece == me)
        def _():
            b_ref[me] = b_tx[me]

    half = count // 2
    start = lax.rem(me // 2 + half // 2, half)
    for k in range(half):
        at = 2 * lax.rem(start + k, half)
        last = lax.rem(at + count - 1, count)
        backs = back_pair(inverse, [spec[1, at], spec[1, at + 1]])
        longs = back_pair(inverse, [spec[0, at], spec[0, at + 1]])
        for p in range(2):
            b_tx[at + p, 0:rows, :] = backs[p]
            b_tx[at + p, rows + TAIL : 2 * rows + TAIL, :] = longs[p]
        b_tx[at, rows : rows + TAIL, :] = backs[1][:TAIL]
        head = backs[0][:TAIL]
        b_tx[last, rows : rows + TAIL, :] = jnp.where(at == 0, jnp.zeros_like(head), head)
        if k > 0:
            give(last)
        give(at)
    give(lax.rem(2 * start + count - 1, count))

    for kind, source, target in ((1, y_tx, y_ref), (2, b_tx, b_ref)):
        for peer in peers:
            arrival(kind, source, target, peer).wait_recv()
    for kind, source, target in ((0, g_tx, g_rx), (1, y_tx, y_ref), (2, b_tx, b_ref)):
        for peer in peers:
            exchange(kind, source, target, peer).wait_send()
    edge.wait()

    @pl.when(me == count - 1)
    def _():
        edge_ref[...] = jnp.zeros_like(edge_ref)


def sum_kernel(part_ref, short_ref, skip_ref, one_rx, total, two_rx, sent, came):
    count = part_ref.shape[0]
    cw = part_ref.shape[2]
    tap_count = short_ref.shape[1]
    me = lax.axis_index("ctx")
    greet("ctx", count, me)
    peers = [lax.rem(me + o, count) for o in far_first(count)]

    def exchange(kind, source, target, peer):
        return send(source, target.at[me], sent.at[kind, peer], came.at[kind, me], peer)

    def arrival(kind, source, target, peer):
        return send(source, target.at[peer], sent.at[kind, peer], came.at[kind, peer], peer)

    for peer in peers:
        exchange(0, part_ref.at[peer], one_rx, peer).start()
    one_rx[me] = part_ref[me]
    for peer in peers:
        arrival(0, part_ref.at[peer], one_rx, peer).wait_recv()
    value = one_rx[0]
    for c in range(1, count):
        value = value + one_rx[c]
    total[...] = value
    for peer in peers:
        exchange(1, total, two_rx, peer).start()
    two_rx[me] = value
    for peer in peers:
        arrival(1, total, two_rx, peer).wait_recv()
    for c in range(count):
        lanes = slice(c * cw, (c + 1) * cw)
        for s in range(3):
            short_ref[s, :, lanes] = two_rx[c, s * tap_count : (s + 1) * tap_count, :]
        skip_ref[:, lanes] = two_rx[c, 3 * tap_count : 3 * tap_count + 1, :]
    for peer in peers:
        exchange(0, part_ref.at[peer], one_rx, peer).wait_send()
        exchange(1, total, two_rx, peer).wait_send()


def leave_kernel(pieces, q_ref, k_ref, v_ref, before, after, go_ref, go_after, taps, skip_ref,
                 y_ref, b_ref, dq_ref, dk_ref, dv_ref, long_ref, sums_ref, ext, go_ext, grad_ext):
    rows, width = q_ref.shape
    cw = width // pieces
    rim = before.shape[1]
    tap_count = taps.shape[1]
    more = rows + PAD
    sums_ref[...] = jnp.zeros_like(sums_ref)
    for c in range(pieces):
        lanes = slice(c * cw, (c + 1) * cw)
        filtered = []
        for s, ref in enumerate((q_ref, k_ref, v_ref)):
            fill(ext.at[s], before[s, :, lanes], ref[:, lanes], after[s, :, lanes], rim)
            filtered.append(short(ext.at[s], taps, more, lanes, s))
        fill(go_ext, jnp.zeros((rim, cw), F32), go_ref[:, lanes], go_after[0:rim, lanes], rim)
        grad_o = go_ext[PAD : PAD + more, :]
        mixed = filtered[1] * filtered[2]
        grad_y = grad_o * filtered[0]
        gain = skip_ref[:, lanes]
        y_full = y_ref[c, 0:more, :].astype(F32) + gain * mixed
        at = rows + TAIL
        grad_mixed = b_ref[c, 0:more, :].astype(F32) + gain * grad_y
        grad_ext[0, 0:more, :] = grad_o * y_full
        grad_ext[1, 0:more, :] = grad_mixed * filtered[2]
        grad_ext[2, 0:more, :] = grad_mixed * filtered[1]
        long_ref[:, lanes] = b_ref[c, at : at + rows, :].astype(F32)
        for s, ref in enumerate((dq_ref, dk_ref, dv_ref)):
            total = None
            own = grad_ext[s, 0:rows, :]
            for j in range(tap_count):
                term = taps[s, j : j + 1, lanes] * grad_ext[s, j : j + rows, :]
                total = term if total is None else total + term
                stream = ext[s, PAD - j : PAD - j + rows, :]
                row = s * tap_count + j
                sums_ref[c, row : row + 1, :] = jnp.sum(own * stream, axis=0, keepdims=True)
            ref[:, lanes] = total.astype(BF16)
        row = 3 * tap_count
        sums_ref[c, row : row + 1, :] = jnp.sum(
            grad_y[0:rows] * mixed[0:rows], axis=0, keepdims=True
        )


def call(kernel, out_shape, scratch, *args, **params):
    return pl.pallas_call(
        kernel,
        out_shape=out_shape,
        in_specs=[pl.BlockSpec(memory_space=pltpu.VMEM)] * len(args),
        out_specs=jax.tree.map(lambda _: pl.BlockSpec(memory_space=pltpu.VMEM), out_shape),
        scratch_shapes=scratch,
        compiler_params=pltpu.CompilerParams(**PARAMS, **params),
    )(*args)


def per_device(queries, keys, values, long_filter, short_filters, skip, w_out, d_out):
    ctx = lax.axis_size("ctx")
    rows, width = queries.shape
    cw = width // ctx
    tap_count = short_filters.shape[1]
    rim = tap_count - 1
    ends = jnp.stack([queries[rows - rim :], keys[rows - rim :], values[rows - rim :]])
    starts = jnp.stack([queries[:rim], keys[:rim], values[:rim]])
    before = shifted(ends, "ctx", 1)
    after = shifted(starts, "ctx", -1)
    before, after = lax.optimization_barrier((before, after))
    ext = pltpu.VMEM((rows + 4 * PAD, cw), F32)
    shape = jax.ShapeDtypeStruct
    mh = call(
        functools.partial(enter_kernel, ctx),
        shape((ctx, 2, rows, cw), BF16), [ext],
        keys, values, before, long_filter, short_filters,
    )
    mh = lax.all_to_all(mh, "ctx", split_axis=0, concat_axis=0, tiled=True)
    grad_o = lax.dot_general(
        lax.all_gather(d_out, "ch", axis=1, tiled=True),
        w_out,
        (((1,), (1,)), ((), ())),
        preferred_element_type=F32,
    ).astype(BF16)
    forward, inverse = tables(rows)
    spare = ctx if ctx > 8 else 1
    one = shape((ctx, rows + TAIL, cw), BF16)
    two = shape((ctx, 2 * rows + TAIL, cw), BF16)
    piece = pltpu.VMEM((ctx, rows, cw), BF16)
    y, back, go_after = call(
        conv_kernel,
        (one, two, shape((TAIL, width), BF16)),
        [ext, piece, piece, pltpu.VMEM(one.shape, BF16), pltpu.VMEM(two.shape, BF16),
         pltpu.VMEM((3, ctx, 2 * rows, cw), F32), pltpu.VMEM((2, spare, 2, 8, cw), F32),
         pltpu.SemaphoreType.DMA((3, ctx)), pltpu.SemaphoreType.DMA((3, ctx)),
         pltpu.SemaphoreType.DMA((2,))],
        queries, before, grad_o, short_filters, mh, jnp.asarray(forward), jnp.asarray(inverse),
        collective_id=1, has_side_effects=True,
    )
    stream = shape((rows, width), BF16)
    dq, dk, dv, d_long, sums = call(
        functools.partial(leave_kernel, ctx),
        (stream, stream, stream, shape((rows, width), F32), shape((ctx, 16, cw), F32)),
        [pltpu.VMEM((3, rows + 4 * PAD, cw), F32), ext, pltpu.VMEM((3, rows + 4 * PAD, cw), F32)],
        queries, keys, values, before, after, grad_o, go_after, short_filters, skip[None], y, back,
    )
    small = pltpu.VMEM((ctx, 16, cw), F32)
    d_short, d_skip = call(
        sum_kernel,
        (shape((3, tap_count, width), F32), shape((1, width), F32)),
        [small, pltpu.VMEM((16, cw), F32), small,
         pltpu.SemaphoreType.DMA((2, ctx)), pltpu.SemaphoreType.DMA((2, ctx))],
        sums,
        collective_id=2, has_side_effects=True,
    )
    return dq, dk, dv, d_long, d_short, d_skip[0]


def solution(mesh):
    in_specs = (
        P("ctx", "ch"),
        P("ctx", "ch"),
        P("ctx", "ch"),
        P("ctx", "ch"),
        P(None, None, "ch"),
        P("ch"),
        P("ch", None),
        P("ctx", "ch"),
    )
    out_specs = (
        P("ctx", "ch"),
        P("ctx", "ch"),
        P("ctx", "ch"),
        P("ctx", "ch"),
        P(None, None, "ch"),
        P("ch"),
    )
    return jax.shard_map(
        per_device, mesh=mesh, in_specs=in_specs, out_specs=out_specs, check_vma=False
    )
```

```python
import functools
import math

import jax
import jax.numpy as jnp
import numpy as np
from jax import lax
from jax.experimental import pallas as pl
from jax.experimental.pallas import tpu as pltpu
from jax.sharding import PartitionSpec as P

PAD = 8
TAIL = 16
PARAMS = dict(vmem_limit_bytes=60 * 1024 * 1024)
F32 = jnp.float32
BF16 = jnp.bfloat16
MESH = pl.DeviceIdType.MESH


def split_table(table):
    table = table.astype(np.float32)
    high = table.astype(BF16)
    low = (table - high.astype(np.float32)).astype(BF16)
    return np.concatenate([high[None], low[None]], axis=0)


def tables(block):
    freq = np.arange(block)[:, None]
    place = np.arange(block)[None, :]
    angle = (2 * freq + 1) * place % (4 * block) * (math.pi / (2 * block))
    forward = np.concatenate([np.cos(angle), -np.sin(angle)], axis=0)
    return split_table(forward), split_table(forward.T / block)


def fill(scratch, before, own, after, rim):
    rows = own.shape[0]
    scratch[0:PAD, :] = jnp.zeros_like(scratch[0:PAD, :])
    scratch[PAD + rows :, :] = jnp.zeros_like(scratch[PAD + rows :, :])
    scratch[PAD - rim : PAD, :] = before.astype(F32)
    scratch[PAD : PAD + rows, :] = own.astype(F32)
    if after is not None:
        scratch[PAD + rows : PAD + rows + rim, :] = after.astype(F32)


def short(scratch, taps, rows, lanes, s):
    total = None
    for j in range(taps.shape[1]):
        term = taps[s, j : j + 1, lanes] * scratch[PAD - j : PAD - j + rows, :]
        total = term if total is None else total + term
    return total


def times(a, b):
    return a[0] * b[0] - a[1] * b[1], a[0] * b[1] + a[1] * b[0]


def conj_times(a, b):
    return a[0] * b[0] + a[1] * b[1], a[0] * b[1] - a[1] * b[0]


def add(a, b):
    return b if a is None else (a[0] + b[0], a[1] + b[1])


def spectra(table, blocks, spec):
    for at in range(0, len(blocks), 2):
        pair = blocks[at : at + 2]
        data = jnp.concatenate([ref[...] for ref, _, _ in pair], axis=1)
        out = jnp.dot(table[0], data, preferred_element_type=F32) + jnp.dot(
            table[1], data, preferred_element_type=F32
        )
        cw = data.shape[1] // len(pair)
        for p, (_, s, i) in enumerate(pair):
            spec[s, i] = out[:, p * cw : (p + 1) * cw]


def mix_spectra(first, spec, held):
    count, rows2, cw = spec.shape[1:]
    half = rows2 // 2
    step = 8
    sign = 1.0 - 2.0 * (lax.broadcasted_iota(jnp.int32, (step, cw), 0) % 2).astype(F32)
    zero = jnp.zeros((step, cw), F32)

    def primes(blocks):
        out = [blocks[0]]
        for d in range(1, count):
            re, im = blocks[d]
            old_re, old_im = blocks[d - 1]
            out.append((re - sign * old_im, im + sign * old_re))
        return out

    def chunk(r, carry):
        low = pl.ds(pl.multiple_of(r * step, step), step)
        high = pl.ds(pl.multiple_of(half + r * step, step), step)

        def load(s, i):
            return spec[s, i, low, :], spec[s, i, high, :]

        def save(s, i, value):
            spec[s, i, low, :] = value[0]
            spec[s, i, high, :] = value[1]

        def primed(s):
            values = primes([load(s, i) for i in range(count)])
            for i in range(count):
                save(s, i, values[i])
            return values

        if count <= 8 and first:
            taps = primed(1)
            mixed = [load(0, i) for i in range(count)]
            for i in range(count):
                total = None
                for d in range(i + 1):
                    total = add(total, times(taps[d], mixed[i - d]))
                save(2, i, total)
            return carry
        if count <= 8:
            grads = [load(2, i) for i in range(count)]
            for s in (1, 0):
                taps = [load(s, i) for i in range(count)]
                if s == 0:
                    taps = primes(taps)
                for b in range(count):
                    total = None
                    for e in range(count - b):
                        total = add(total, conj_times(taps[e], grads[b + e]))
                    save(s, b, total)
            return carry
        if first:
            primed(1)

            def one(b, inner):
                def of_y(d, total):
                    return add(total, times(load(1, d), load(0, b - d)))

                save(2, b, lax.fori_loop(0, b + 1, of_y, (zero, zero)))
                return inner

            lax.fori_loop(0, count, one, 0)
            return carry
        primed(0)

        def both(b, inner):
            def of_g(e, totals):
                grad = load(2, b + e)
                return (
                    add(totals[0], conj_times(load(1, e), grad)),
                    add(totals[1], conj_times(load(0, e), grad)),
                )

            pair = lax.fori_loop(0, count - b, of_g, ((zero, zero), (zero, zero)))
            for s in range(2):
                held[s, b, 0], held[s, b, 1] = pair[s]
            return inner

        lax.fori_loop(0, count, both, 0)
        for b in range(count):
            save(1, b, (held[0, b, 0], held[0, b, 1]))
            save(0, b, (held[1, b, 0], held[1, b, 1]))
        return carry

    lax.fori_loop(0, half // step, chunk, 0)


def back_pair(table, values):
    data = jnp.concatenate(values, axis=1)
    high = data.astype(BF16)
    low = (data - high.astype(F32)).astype(BF16)
    out = (
        jnp.dot(table[0], high, preferred_element_type=F32)
        + jnp.dot(table[0], low, preferred_element_type=F32)
        + jnp.dot(table[1], high, preferred_element_type=F32)
    )
    cw = data.shape[1] // len(values)
    return [out[:, p * cw : (p + 1) * cw].astype(BF16) for p in range(len(values))]


def greet(sizes):
    barrier = pltpu.get_barrier_semaphore()
    for axis, size in sizes:
        me = lax.axis_index(axis)
        for o in range(1, size):
            peer = lax.rem(me + o, size)
            pl.semaphore_signal(barrier, inc=1, device_id={axis: peer}, device_id_type=MESH)
    pl.semaphore_wait(barrier, sum(size - 1 for _, size in sizes))


def send(source, target, send_sem, recv_sem, peer, axis="ctx"):
    return pltpu.make_async_remote_copy(
        src_ref=source,
        dst_ref=target,
        send_sem=send_sem,
        recv_sem=recv_sem,
        device_id={axis: peer},
        device_id_type=MESH,
    )


def far_first(size):
    return sorted(range(1, size), key=lambda o: abs(o - size // 2))


def gather_kernel(q_ref, k_ref, v_ref, long_ref, taps, d_ref, w_hbm,
                  mh_ref, go_ref, before, after, ext, mh_tx, held, weights, total,
                  edge_sent, edge_came, sent, came, own_sent, pass_sent, d_came, w_sem):
    count, _, rows, cw = mh_ref.shape
    parts, halves = held.shape[:2]
    cols = d_ref.shape[1]
    piece = cols // halves
    rim = taps.shape[1] - 1
    me = lax.axis_index("ctx")
    mine = lax.axis_index("ch")
    partner = mine + 1 - 2 * lax.rem(mine, 2)
    greet([("ctx", count), ("ch", parts)])

    rest = [lax.rem(mine + 2 * o, parts) for o in range(1, parts // 2)]
    other = [lax.rem(partner + 2 * o, parts) for o in range(1, parts // 2)]
    after_me = lax.rem(me + 1, count)
    before_me = lax.rem(me + count - 1, count)

    edges = []
    for s, ref in ((1, k_ref), (2, v_ref), (0, q_ref)):
        edges.append(send(ref.at[rows - TAIL : rows], before.at[s], edge_sent.at[s],
                          edge_came.at[s], after_me))
    for s, ref in ((0, q_ref), (1, k_ref), (2, v_ref)):
        edges.append(send(ref.at[0:TAIL], after.at[s], edge_sent.at[3 + s],
                          edge_came.at[3 + s], before_me))
    for edge in edges:
        edge.start()

    def own(slot, half, peer):
        lanes = slice(half * piece, (half + 1) * piece)
        return send(d_ref.at[:, lanes], held.at[mine, half], own_sent.at[slot, half],
                    d_came.at[mine, half], peer, "ch")

    def passed(slot, half, part):
        return send(held.at[part, half], held.at[part, half], pass_sent.at[slot, half],
                    d_came.at[part, half], partner, "ch")

    for half in range(halves):
        for slot, peer in enumerate(rest + [partner]):
            own(slot, half, peer).start()

    def weight(part):
        lanes = pl.ds(pl.multiple_of(part * cols, cols), cols)
        return pltpu.make_async_copy(w_hbm.at[:, lanes], weights.at[part], w_sem.at[part])

    order = [mine, partner] + [p for pair in zip(rest, other) for p in pair]
    for part in order:
        weight(part).start()
    for edge in edges:
        edge.wait()

    @pl.when(me == 0)
    def _():
        before[...] = jnp.zeros_like(before)

    @pl.when(me == count - 1)
    def _():
        after[...] = jnp.zeros_like(after)

    for c in range(count):
        lanes = slice(c * cw, (c + 1) * cw)
        fill(ext, before[1, TAIL - rim :, lanes], k_ref[:, lanes], None, rim)
        keyed = short(ext, taps, rows, lanes, 1)
        fill(ext, before[2, TAIL - rim :, lanes], v_ref[:, lanes], None, rim)
        mh_tx[c, 0] = (keyed * short(ext, taps, rows, lanes, 2)).astype(BF16)
        mh_tx[c, 1] = long_ref[:, lanes].astype(BF16)

    def exchange(peer):
        return send(mh_tx.at[peer], mh_ref.at[me], sent.at[peer], came.at[me], peer)

    def arrival(peer):
        return send(mh_tx.at[peer], mh_ref.at[peer], sent.at[peer], came.at[peer], peer)

    peers = [lax.rem(me + o, count) for o in far_first(count)]
    for peer in peers:
        exchange(peer).start()
    mh_ref[me] = mh_tx[me]

    def product(data, part, half=None):
        lanes = slice(None) if half is None else slice(half * piece, (half + 1) * piece)
        return lax.dot_general(data, weights[part, :, lanes], (((1,), (1,)), ((), ())),
                               preferred_element_type=F32)

    def take(part, half):
        total[...] += product(held[part, half], part, half)

    weight(mine).wait()
    total[...] = product(d_ref[...], mine)
    weight(partner).wait()
    for half in range(halves):
        passed(0, half, partner).wait_recv()
        take(partner, half)
    for slot, (direct, relayed) in enumerate(zip(rest, other)):
        weight(direct).wait()
        weight(relayed).wait()
        for half in range(halves):
            passed(slot, half, direct).wait_recv()
            passed(slot, half, direct).start()
            take(direct, half)
            passed(slot, half, relayed).wait_recv()
            take(relayed, half)
    go_ref[...] = total[...].astype(BF16)

    for peer in peers:
        arrival(peer).wait_recv()
    for peer in peers:
        exchange(peer).wait_send()
    for half in range(halves):
        for slot, peer in enumerate(rest + [partner]):
            own(slot, half, peer).wait_send()
        for slot, direct in enumerate(rest):
            passed(slot, half, direct).wait_send()


def conv_kernel(q_ref, before, go_ref, taps, mh_ref, forward, inverse, y_ref, b_ref, edge_ref,
                ext, g_tx, g_rx, y_tx, b_tx, spec, held, sent, came, edge_sem):
    count, _, rows, cw = mh_ref.shape
    rim = taps.shape[1] - 1
    me = lax.axis_index("ctx")
    greet([("ctx", count)])
    edge_rows = edge_ref.shape[0]
    previous = lax.rem(me + count - 1, count)
    edge = send(go_ref.at[0:edge_rows], edge_ref, edge_sem.at[0], edge_sem.at[1], previous)
    edge.start()
    for c in range(count):
        lanes = slice(c * cw, (c + 1) * cw)
        fill(ext, before[0, TAIL - rim :, lanes], q_ref[:, lanes], None, rim)
        g_tx[c] = (go_ref[:, lanes].astype(F32) * short(ext, taps, rows, lanes, 0)).astype(BF16)

    def exchange(kind, source, target, peer):
        return send(
            source.at[peer], target.at[me], sent.at[kind, peer], came.at[kind, me], peer
        )

    def arrival(kind, source, target, peer):
        return send(
            source.at[peer], target.at[peer], sent.at[kind, peer], came.at[kind, peer], peer
        )

    peers = [lax.rem(me + o, count) for o in far_first(count)]
    for peer in peers:
        exchange(0, g_tx, g_rx, peer).start()
    g_rx[me] = g_tx[me]

    blocks = []
    for i in range(count):
        blocks += [(mh_ref.at[i, 0], 0, i), (mh_ref.at[i, 1], 1, i)]
    spectra(forward, blocks, spec)
    mix_spectra(True, spec, held)
    for i in range(0, count, 2):
        for p, value in enumerate(back_pair(inverse, [spec[2, i], spec[2, i + 1]])):
            y_tx[i + p, 0:rows, :] = value
            if i + p > 0:
                y_tx[i + p - 1, rows : rows + TAIL, :] = value[:TAIL]
    y_tx[count - 1, rows : rows + TAIL, :] = jnp.zeros((TAIL, cw), BF16)
    for peer in peers:
        exchange(1, y_tx, y_ref, peer).start()
    y_ref[me] = y_tx[me]

    for peer in peers:
        arrival(0, g_tx, g_rx, peer).wait_recv()
    spectra(forward, [(g_rx.at[i], 2, i) for i in range(count)], spec)
    mix_spectra(False, spec, held)

    def give(piece):
        @pl.when(piece != me)
        def _():
            exchange(2, b_tx, b_ref, piece).start()

        @pl.when(piece == me)
        def _():
            b_ref[me] = b_tx[me]

    half = count // 2
    start = lax.rem(me // 2 + half // 2, half)
    for k in range(half):
        at = 2 * lax.rem(start + k, half)
        last = lax.rem(at + count - 1, count)
        backs = back_pair(inverse, [spec[1, at], spec[1, at + 1]])
        longs = back_pair(inverse, [spec[0, at], spec[0, at + 1]])
        for p in range(2):
            b_tx[at + p, 0:rows, :] = backs[p]
            b_tx[at + p, rows + TAIL : 2 * rows + TAIL, :] = longs[p]
        b_tx[at, rows : rows + TAIL, :] = backs[1][:TAIL]
        head = backs[0][:TAIL]
        b_tx[last, rows : rows + TAIL, :] = jnp.where(at == 0, jnp.zeros_like(head), head)
        if k > 0:
            give(last)
        give(at)
    give(lax.rem(2 * start + count - 1, count))

    for kind, source, target in ((1, y_tx, y_ref), (2, b_tx, b_ref)):
        for peer in peers:
            arrival(kind, source, target, peer).wait_recv()
    for kind, source, target in ((0, g_tx, g_rx), (1, y_tx, y_ref), (2, b_tx, b_ref)):
        for peer in peers:
            exchange(kind, source, target, peer).wait_send()
    edge.wait()

    @pl.when(me == count - 1)
    def _():
        edge_ref[...] = jnp.zeros_like(edge_ref)


def sum_kernel(part_ref, short_ref, skip_ref, one_rx, total, two_rx, sent, came):
    count = part_ref.shape[0]
    cw = part_ref.shape[2]
    tap_count = short_ref.shape[1]
    me = lax.axis_index("ctx")
    greet([("ctx", count)])
    peers = [lax.rem(me + o, count) for o in far_first(count)]

    def exchange(kind, source, target, peer):
        return send(source, target.at[me], sent.at[kind, peer], came.at[kind, me], peer)

    def arrival(kind, source, target, peer):
        return send(source, target.at[peer], sent.at[kind, peer], came.at[kind, peer], peer)

    for peer in peers:
        exchange(0, part_ref.at[peer], one_rx, peer).start()
    one_rx[me] = part_ref[me]
    for peer in peers:
        arrival(0, part_ref.at[peer], one_rx, peer).wait_recv()
    value = one_rx[0]
    for c in range(1, count):
        value = value + one_rx[c]
    total[...] = value
    for peer in peers:
        exchange(1, total, two_rx, peer).start()
    two_rx[me] = value
    for peer in peers:
        arrival(1, total, two_rx, peer).wait_recv()
    for c in range(count):
        lanes = slice(c * cw, (c + 1) * cw)
        for s in range(3):
            short_ref[s, :, lanes] = two_rx[c, s * tap_count : (s + 1) * tap_count, :]
        skip_ref[:, lanes] = two_rx[c, 3 * tap_count : 3 * tap_count + 1, :]
    for peer in peers:
        exchange(0, part_ref.at[peer], one_rx, peer).wait_send()
        exchange(1, total, two_rx, peer).wait_send()


def leave_kernel(pieces, q_ref, k_ref, v_ref, before, after, go_ref, go_after, taps, skip_ref,
                 y_ref, b_ref, dq_ref, dk_ref, dv_ref, long_ref, sums_ref, ext, go_ext, grad_ext):
    rows, width = q_ref.shape
    cw = width // pieces
    rim = taps.shape[1] - 1
    tap_count = taps.shape[1]
    more = rows + PAD
    sums_ref[...] = jnp.zeros_like(sums_ref)
    for c in range(pieces):
        lanes = slice(c * cw, (c + 1) * cw)
        filtered = []
        for s, ref in enumerate((q_ref, k_ref, v_ref)):
            fill(ext.at[s], before[s, TAIL - rim :, lanes], ref[:, lanes], after[s, 0:rim, lanes], rim)
            filtered.append(short(ext.at[s], taps, more, lanes, s))
        fill(go_ext, jnp.zeros((rim, cw), F32), go_ref[:, lanes], go_after[0:rim, lanes], rim)
        grad_o = go_ext[PAD : PAD + more, :]
        mixed = filtered[1] * filtered[2]
        grad_y = grad_o * filtered[0]
        gain = skip_ref[:, lanes]
        y_full = y_ref[c, 0:more, :].astype(F32) + gain * mixed
        at = rows + TAIL
        grad_mixed = b_ref[c, 0:more, :].astype(F32) + gain * grad_y
        grad_ext[0, 0:more, :] = grad_o * y_full
        grad_ext[1, 0:more, :] = grad_mixed * filtered[2]
        grad_ext[2, 0:more, :] = grad_mixed * filtered[1]
        long_ref[:, lanes] = b_ref[c, at : at + rows, :].astype(F32)
        for s, ref in enumerate((dq_ref, dk_ref, dv_ref)):
            total = None
            own = grad_ext[s, 0:rows, :]
            for j in range(tap_count):
                term = taps[s, j : j + 1, lanes] * grad_ext[s, j : j + rows, :]
                total = term if total is None else total + term
                stream = ext[s, PAD - j : PAD - j + rows, :]
                row = s * tap_count + j
                sums_ref[c, row : row + 1, :] = jnp.sum(own * stream, axis=0, keepdims=True)
            ref[:, lanes] = total.astype(BF16)
        row = 3 * tap_count
        sums_ref[c, row : row + 1, :] = jnp.sum(
            grad_y[0:rows] * mixed[0:rows], axis=0, keepdims=True
        )


def call(kernel, out_shape, scratch, *args, hbm=(), **params):
    vmem = pl.BlockSpec(memory_space=pltpu.VMEM)
    return pl.pallas_call(
        kernel,
        out_shape=out_shape,
        in_specs=[pl.BlockSpec(memory_space=pl.ANY) if i in hbm else vmem
                  for i in range(len(args))],
        out_specs=jax.tree.map(lambda _: vmem, out_shape),
        scratch_shapes=scratch,
        compiler_params=pltpu.CompilerParams(**PARAMS, **params),
    )(*args)


def per_device(queries, keys, values, long_filter, short_filters, skip, w_out, d_out):
    ctx = lax.axis_size("ctx")
    rows, width = queries.shape
    cw = width // ctx
    tap_count = short_filters.shape[1]
    parts = lax.axis_size("ch")
    cols = d_out.shape[1]
    halves = 2
    ext = pltpu.VMEM((rows + 4 * PAD, cw), F32)
    shape = jax.ShapeDtypeStruct
    dma = pltpu.SemaphoreType.DMA
    edge = shape((3, TAIL, width), BF16)
    pair = (ctx, 2, rows, cw)
    mh, grad_o, before, after = call(
        gather_kernel,
        (shape(pair, BF16), shape((rows, width), BF16), edge, edge),
        [ext, pltpu.VMEM(pair, BF16), pltpu.VMEM((parts, halves, rows, cols // halves), BF16),
         pltpu.VMEM((parts, width, cols), BF16), pltpu.VMEM((rows, width), F32),
         dma((6,)), dma((6,)), dma((ctx,)), dma((ctx,)), dma((parts // 2, halves)),
         dma((parts // 2, halves)), dma((parts, halves)), dma((parts,))],
        queries, keys, values, long_filter, short_filters, d_out, w_out,
        hbm=(6,), collective_id=3, has_side_effects=True,
    )
    forward, inverse = tables(rows)
    spare = ctx if ctx > 8 else 1
    one = shape((ctx, rows + TAIL, cw), BF16)
    two = shape((ctx, 2 * rows + TAIL, cw), BF16)
    piece = pltpu.VMEM((ctx, rows, cw), BF16)
    y, back, go_after = call(
        conv_kernel,
        (one, two, shape((TAIL, width), BF16)),
        [ext, piece, piece, pltpu.VMEM(one.shape, BF16), pltpu.VMEM(two.shape, BF16),
         pltpu.VMEM((3, ctx, 2 * rows, cw), F32), pltpu.VMEM((2, spare, 2, 8, cw), F32),
         pltpu.SemaphoreType.DMA((3, ctx)), pltpu.SemaphoreType.DMA((3, ctx)),
         pltpu.SemaphoreType.DMA((2,))],
        queries, before, grad_o, short_filters, mh, jnp.asarray(forward), jnp.asarray(inverse),
        collective_id=1, has_side_effects=True,
    )
    stream = shape((rows, width), BF16)
    dq, dk, dv, d_long, sums = call(
        functools.partial(leave_kernel, ctx),
        (stream, stream, stream, shape((rows, width), F32), shape((ctx, 16, cw), F32)),
        [pltpu.VMEM((3, rows + 4 * PAD, cw), F32), ext, pltpu.VMEM((3, rows + 4 * PAD, cw), F32)],
        queries, keys, values, before, after, grad_o, go_after, short_filters, skip[None], y, back,
    )
    small = pltpu.VMEM((ctx, 16, cw), F32)
    d_short, d_skip = call(
        sum_kernel,
        (shape((3, tap_count, width), F32), shape((1, width), F32)),
        [small, pltpu.VMEM((16, cw), F32), small,
         pltpu.SemaphoreType.DMA((2, ctx)), pltpu.SemaphoreType.DMA((2, ctx))],
        sums,
        collective_id=2, has_side_effects=True,
    )
    return dq, dk, dv, d_long, d_short, d_skip[0]


def solution(mesh):
    in_specs = (
        P("ctx", "ch"),
        P("ctx", "ch"),
        P("ctx", "ch"),
        P("ctx", "ch"),
        P(None, None, "ch"),
        P("ch"),
        P("ch", None),
        P("ctx", "ch"),
    )
    out_specs = (
        P("ctx", "ch"),
        P("ctx", "ch"),
        P("ctx", "ch"),
        P("ctx", "ch"),
        P(None, None, "ch"),
        P("ch"),
    )
    return jax.shard_map(
        per_device, mesh=mesh, in_specs=in_specs, out_specs=out_specs, check_vma=False
    )
```
